256 devices in a mesh: segment: 16 (over z, core), node: 16 (over y, x).
Axes of the slice: x: 4, y: 4, z: 8, core: 2. Of those that a mesh axis runs over, the one named last changes fastest.
Arguments:
- features: bfloat16 [2, 8192, 256], P(None, 'node'), may hold values from -6 to 6
- tiles: bfloat16 [2, 64, 8, 128, 128], P(None, 'node'), may hold values from -0.25 to 0.25
- tile_cols: int32 [2, 64, 8], P(None, 'node'), may hold values from 0 to 63, as said below
- tile_count: int32 [2, 64], P(None, 'node'), may hold values from 1 to 8
- weights: bfloat16 [16, 256, 256], P('segment'), may hold values from -0.375 to 0.375
Outputs:
- layer_outputs: bfloat16 [16, 2, 8192, 256], P('segment', None, 'node')
The draws below stay inside these ranges and needn't reach their ends.
Inputs may be any that keep to these rules, and one draw needn't show every extreme that they name: `tile_cols`: with P = 4 block rows per node group of 512 nodes, the block column of a tile in block row b lies in group g - 1, g or g + 1 (counted modulo 8192 / 512 groups) where g = b // P is the group of b. `tile_count`: slots from the count on are padding.
All inputs are finite; a program needn't handle non-finite values.
Results may differ from the reference program's by a relative error of at most 0.011.
Values may be sent and summed in bfloat16 or wider, within the bound.
No kernel may reach another device: no remote copies, remote signals or barrier semaphores. Data moves between devices by JAX's collectives and lax.ppermute only.
A program may use at most 64 MiB of HBM per device.

```python
import jax
import jax.numpy as jnp
from jax import lax

D = 256
TILE = 128
SLOTS = 8
SPANS = 2
ROWS_DEV = 512
LAYERS = 16
SPAN = 8192
NB = 64
N_NODE = 16


def draw_tile_cols(key, part):
    per_group = ROWS_DEV // TILE
    key_side, key_inner = jax.random.split(jax.random.fold_in(key, 17))
    side = jax.random.randint(key_side, (SPANS, NB, SLOTS), -1, 2, dtype=jnp.int32)
    inner = jax.random.randint(key_inner, (SPANS, NB, SLOTS), 0, per_group, dtype=jnp.int32)
    owner = jnp.arange(NB, dtype=jnp.int32) // per_group
    group = (owner[None, :, None] + side + N_NODE) % N_NODE
    return (group * per_group + inner).astype(jnp.int32)


def plant(result, rng, low, high):
    spot = [jax.random.randint(jax.random.fold_in(rng, axis), (), 0, length) for axis, length in enumerate(result.shape)]
    longest = result.shape.index(max(result.shape))
    beside = spot[:longest] + [(spot[longest] + 1) % result.shape[longest]] + spot[longest + 1:]
    return result.at[tuple(spot)].set(low).at[tuple(beside)].set(high)


def level_of(key, extent, pieces, smallest, top_value):
    def one(dim, blocks):
        draws = jax.random.uniform(jax.random.fold_in(jax.random.fold_in(key, 6), dim), (blocks,), jnp.float32, smallest / len(pieces), top_value / len(pieces))
        return jnp.repeat(jnp.exp(draws), extent[dim] // blocks).reshape((-1,) + (1,) * (len(extent) - dim - 1))

    loudness = one(*pieces[0])
    for cut in pieces[1:]:
        loudness = loudness * one(*cut)
    return loudness


def bell_draw(own_key, dims, deviation, most, cuts=(), kind=jnp.bfloat16):
    result = deviation * jax.random.normal(own_key, dims, jnp.float32)
    if cuts:
        result = result * level_of(own_key, dims, cuts, -0.22, 0.18)
    return jnp.clip(result, -most, most).astype(kind)


def setup_inputs(seed: int = 0) -> dict:
    splits = jax.random.split(jax.random.key(seed), 6)
    return {
        "features": bell_draw(splits[0], (SPANS, SPAN, D), 1.0, 6.0, ((1, 16),)),
        "tiles": bell_draw(splits[1], (SPANS, NB, SLOTS, TILE, TILE), (4 * TILE) ** -0.5, 0.25, ((1, 16),)),
        "tile_cols": draw_tile_cols(jax.random.fold_in(splits[5], 71), 0),
        "tile_count": plant(jax.random.randint(splits[3], (SPANS, NB), 1, SLOTS + 1), jax.random.fold_in(splits[3], 1), 1, SLOTS).astype(jnp.int32),
        "weights": bell_draw(splits[4], (LAYERS, D, D), D ** -0.5, 0.375, ((0, 16),)),
    }


def layer_rows(hidden, masked, columns, initial, weight, beta_mix):
    grouped = hidden.reshape(NB, TILE, D)
    picked = grouped[columns]
    aggregate = jnp.einsum("bkij,bkjd->bid", masked.astype(jnp.float32), picked.astype(jnp.float32)).reshape(SPAN, D)
    support = (0.9 * aggregate + 0.1 * initial.astype(jnp.float32)).astype(jnp.bfloat16)
    branch = jnp.dot(support, weight, preferred_element_type=jnp.float32)
    combined = (1.0 - beta_mix) * support.astype(jnp.float32) + beta_mix * branch
    return jnp.maximum(combined, 0.0).astype(jnp.bfloat16)


def reference(features, tiles, tile_cols, tile_count, weights):
    slot_ids = jnp.arange(SLOTS, dtype=jnp.int32)
    live = (slot_ids[None, None, :] < tile_count[:, :, None]).astype(jnp.bfloat16)
    masked = tiles * live[:, :, :, None, None]
    layer_ids = jnp.arange(LAYERS, dtype=jnp.float32)
    betas = jnp.log(0.5 / (layer_ids + 1.0) + 1.0)

    def one_layer(hidden, inputs):
        weight, beta_mix = inputs
        results = jnp.stack([layer_rows(hidden[k], masked[k], tile_cols[k], features[k], weight, beta_mix) for k in range(SPANS)])
        return results, results

    final, stacked = lax.scan(one_layer, features, (weights, betas))
    return stacked
```

```python
import math

import jax
import jax.numpy as jnp
from jax import lax
from jax.experimental import pallas as pl
from jax.experimental.pallas import tpu as pltpu
from jax.sharding import PartitionSpec as P

BLOCK = 128
HALF = 256
VMEM = pl.BlockSpec(memory_space=pltpu.VMEM)
SMEM = pl.BlockSpec(memory_space=pltpu.SMEM)


def dense_kernel(places_ref, tiles_ref, dense_ref, total_ref):
    total_ref[...] = jnp.zeros_like(total_ref)
    blocks, slots = places_ref.shape
    for b in range(blocks):
        rows = pl.ds(b * BLOCK, BLOCK)
        for k in range(slots):
            place = places_ref[b, k]
            chunk = place // 2
            tile = tiles_ref[pl.ds((b * slots + k) * BLOCK, BLOCK), :].astype(jnp.float32)

            @pl.when((place < 12) & (place % 2 == 0))
            def _():
                total_ref[chunk, rows, 0:BLOCK] += tile

            @pl.when((place < 12) & (place % 2 == 1))
            def _():
                total_ref[chunk, rows, BLOCK:HALF] += tile

    dense_ref[...] = total_ref[...].astype(jnp.bfloat16)


def dense_adjacency(places, tiles):
    rows = places.shape[0] * BLOCK
    return pl.pallas_call(
        dense_kernel,
        out_shape=jax.ShapeDtypeStruct((6, rows, HALF), jnp.bfloat16),
        in_specs=[SMEM, VMEM],
        out_specs=VMEM,
        scratch_shapes=[pltpu.VMEM((6, rows, HALF), jnp.float32)],
        compiler_params=pltpu.CompilerParams(vmem_limit_bytes=16 << 20),
    )(places, tiles)


def product(dense_ref, chunk, rows_ref):
    first = jnp.dot(dense_ref[chunk], rows_ref[0:HALF, :], preferred_element_type=jnp.float32)
    second = jnp.dot(dense_ref[chunk + 1], rows_ref[HALF:, :], preferred_element_type=jnp.float32)
    return first + second


def own_kernel(dense_ref, own_ref, part_ref):
    part_ref[...] = product(dense_ref, 0, own_ref)


def own_part(dense, own):
    return pl.pallas_call(
        own_kernel,
        out_shape=jax.ShapeDtypeStruct(own.shape, jnp.float32),
        in_specs=[VMEM, VMEM],
        out_specs=VMEM,
        cost_estimate=pl.CostEstimate(flops=2 * 512 * 512 * 256, bytes_accessed=1 << 20, transcendentals=0),
    )(dense, own)


def layer_kernel(beta, dense_ref, part_ref, beside_ref, across_ref, initial_ref, weight_ref, out_ref):
    aggregate = part_ref[...] + product(dense_ref, 2, beside_ref)
    aggregate = aggregate + product(dense_ref, 4, across_ref)
    support = (0.9 * aggregate + 0.1 * initial_ref[...].astype(jnp.float32)).astype(jnp.bfloat16)
    branch = jnp.dot(support, weight_ref[...], preferred_element_type=jnp.float32)
    combined = (1.0 - beta) * support.astype(jnp.float32) + beta * branch
    out_ref[...] = jnp.maximum(combined, 0.0).astype(jnp.bfloat16)


def layer(beta, dense, part, beside, across, initial, weight):
    return pl.pallas_call(
        lambda *refs: layer_kernel(beta, *refs),
        out_shape=jax.ShapeDtypeStruct(initial.shape, jnp.bfloat16),
        in_specs=[VMEM] * 6,
        out_specs=VMEM,
        cost_estimate=pl.CostEstimate(flops=2 * 512 * 1280 * 256, bytes_accessed=2 << 20, transcendentals=0),
    )(dense, part, beside, across, initial, weight)


def on_device(features, tiles, tile_cols, tile_count, weights):
    groups = lax.axis_size("node")
    layers = lax.axis_size("segment")
    seg = lax.axis_index("segment")
    node = lax.axis_index("node")
    per_group, slots = tile_cols.shape[1:]
    core = seg % 2
    both = ("segment", "node")
    turn = [(s * groups + n, n * groups + s) for s in range(layers) for n in range(groups)]
    pairs_beside = [(s, s ^ 1) for s in range(layers)]
    pairs_across = [(s, (s + 1) % layers if s % 2 else (s - 1) % layers) for s in range(layers)]

    all_weights = lax.all_gather(weights[0], "segment", axis=0, tiled=False)

    cols = lax.dynamic_index_in_dim(tile_cols, core, 0, keepdims=False)
    count = lax.dynamic_index_in_dim(tile_count, core, 0, keepdims=False)
    relative = (cols - (node - 1) * per_group) % (per_group * groups)
    side = relative // per_group
    odd = node % 2
    part_of = jnp.where(side == 1, 0, jnp.where((side == 2) == (odd == 0), 1, 2))
    places = part_of * per_group + relative % per_group
    places = jnp.where(jnp.arange(slots, dtype=jnp.int32)[None, :] < count[:, None], places, 12)
    note = jnp.zeros((16, BLOCK), jnp.bfloat16).at[0:per_group, 0:slots].set(places.astype(jnp.bfloat16))

    mine = lax.dynamic_index_in_dim(features, core, 0, keepdims=False)
    mine_tiles = lax.dynamic_index_in_dim(tiles, core, 0, keepdims=False).reshape(-1, BLOCK)
    bundle = jnp.concatenate([mine_tiles, mine[:, :BLOCK], mine[:, BLOCK:], note], axis=0)
    bundle = lax.ppermute(bundle, both, turn)

    tile_rows = mine_tiles.shape[0]
    rows = mine.shape[0]
    held_tiles = bundle[:tile_rows]
    initial = jnp.concatenate(
        [bundle[tile_rows : tile_rows + rows], bundle[tile_rows + rows : tile_rows + 2 * rows]], axis=1
    )
    held_places = bundle[tile_rows + 2 * rows :][0:per_group, 0:slots].astype(jnp.int32)
    dense = dense_adjacency(held_places, held_tiles)

    hidden = initial
    kept = [initial, initial]
    low = node - node % 2
    for step in range(layers):
        beta = math.log(0.5 / (step + 1) + 1.0)
        across = lax.ppermute(hidden, "segment", pairs_across)
        beside = lax.ppermute(hidden, "segment", pairs_beside)
        part = own_part(dense, hidden)
        hidden = layer(beta, dense, part, beside, across, initial, all_weights[step])
        kept[step % 2] = jnp.where(low == step - step % 2, hidden, kept[step % 2])

    arrived = lax.ppermute(jnp.stack(kept), both, turn)
    mine_out = lax.dynamic_index_in_dim(arrived, core, 0, keepdims=False)
    give = lax.dynamic_index_in_dim(arrived, 1 - core, 0, keepdims=False)
    other = lax.ppermute(give, "segment", pairs_beside)
    first = jnp.where(core == 0, mine_out, other)
    second = jnp.where(core == 0, other, mine_out)
    return jnp.stack([first, second])[None]


def solution(mesh):
    in_specs = (
        P(None, "node", None),
        P(None, "node", None, None, None),
        P(None, "node", None),
        P(None, "node"),
        P("segment", None, None),
    )
    out_specs = P("segment", None, "node", None)
    return jax.shard_map(
        on_device, mesh=mesh, in_specs=in_specs, out_specs=out_specs, check_vma=False
    )
```

```python
import math

import jax
import jax.numpy as jnp
from jax import lax
from jax.experimental import pallas as pl
from jax.experimental.pallas import tpu as pltpu
from jax.sharding import PartitionSpec as P

BLOCK = 128
HALF = 256
VMEM = pl.BlockSpec(memory_space=pltpu.VMEM)
SMEM = pl.BlockSpec(memory_space=pltpu.SMEM)


def dense_kernel(places_ref, tiles_ref, own_ref, before_ref, after_ref, total_ref):
    total_ref[...] = jnp.zeros_like(total_ref)
    blocks, slots = places_ref.shape
    for b in range(blocks):
        rows = pl.ds(b * BLOCK, BLOCK)

        @pl.loop(0, slots)
        def _(k):
            place = places_ref[b, k]
            chunk = place // 2
            tile = tiles_ref[b * slots + k].astype(jnp.float32)

            @pl.when((place < 12) & (place % 2 == 0))
            def _():
                total_ref[chunk, rows, 0:BLOCK] += tile

            @pl.when((place < 12) & (place % 2 == 1))
            def _():
                total_ref[chunk, rows, BLOCK:HALF] += tile

    own_ref[...] = total_ref[0:2].astype(jnp.bfloat16)
    before_ref[...] = total_ref[2:4].astype(jnp.bfloat16)
    after_ref[...] = total_ref[4:6].astype(jnp.bfloat16)


def dense_adjacency(places, tiles):
    rows = places.shape[0] * BLOCK
    part = jax.ShapeDtypeStruct((2, rows, HALF), jnp.bfloat16)
    return pl.pallas_call(
        dense_kernel,
        out_shape=(part, part, part),
        in_specs=[SMEM, VMEM],
        out_specs=(VMEM, VMEM, VMEM),
        scratch_shapes=[pltpu.VMEM((6, rows, HALF), jnp.float32)],
        compiler_params=pltpu.CompilerParams(vmem_limit_bytes=16 << 20),
    )(places, tiles)


def product(dense_ref, rows_ref, rows=slice(None)):
    first = jnp.dot(dense_ref[0, rows, :], rows_ref[0:HALF, :], preferred_element_type=jnp.float32)
    second = jnp.dot(dense_ref[1, rows, :], rows_ref[HALF:, :], preferred_element_type=jnp.float32)
    return first + second


def own_kernel(dense_ref, own_ref, part_ref):
    @pl.loop(0, 4)
    def _(r):
        rows = pl.ds(pl.multiple_of(r * BLOCK, BLOCK), BLOCK)
        part_ref[rows, :] = product(dense_ref, own_ref, rows)


def own_part(dense, own):
    return pl.pallas_call(
        own_kernel,
        out_shape=jax.ShapeDtypeStruct(own.shape, jnp.float32),
        in_specs=[VMEM, VMEM],
        out_specs=VMEM,
        compiler_params=pltpu.CompilerParams(vmem_limit_bytes=12 << 20),
        cost_estimate=pl.CostEstimate(flops=2 * 512 * 512 * 256, bytes_accessed=1 << 20, transcendentals=0),
    )(dense, own)


def layer_kernel(beta, to_before_ref, to_after_ref, part_ref, before_ref, after_ref, initial_ref, weight_ref, out_ref):
    aggregate = part_ref[...] + product(to_before_ref, before_ref)
    aggregate = aggregate + product(to_after_ref, after_ref)
    support = (0.9 * aggregate + 0.1 * initial_ref[...].astype(jnp.float32)).astype(jnp.bfloat16)
    branch = jnp.dot(support, weight_ref[...], preferred_element_type=jnp.float32)
    combined = (1.0 - beta) * support.astype(jnp.float32) + beta * branch
    out_ref[...] = jnp.maximum(combined, 0.0).astype(jnp.bfloat16)


def layer(beta, to_before, to_after, part, before, after, initial, weight):
    return pl.pallas_call(
        lambda *refs: layer_kernel(beta, *refs),
        out_shape=jax.ShapeDtypeStruct(initial.shape, jnp.bfloat16),
        in_specs=[VMEM] * 7,
        out_specs=VMEM,
        compiler_params=pltpu.CompilerParams(vmem_limit_bytes=12 << 20),
        cost_estimate=pl.CostEstimate(flops=2 * 512 * 1280 * 256, bytes_accessed=2 << 20, transcendentals=0),
    )(to_before, to_after, part, before, after, initial, weight)


def on_device(features, tiles, tile_cols, tile_count, weights):
    groups = lax.axis_size("node")
    layers = lax.axis_size("segment")
    seg = lax.axis_index("segment")
    node = lax.axis_index("node")
    per_group, slots = tile_cols.shape[1:]
    core = seg % 2
    up = [(n, (n + 1) % groups) for n in range(groups)]
    down = [(n, (n - 1) % groups) for n in range(groups)]
    swap = [(s, s ^ 1) for s in range(layers)]

    all_weights = lax.all_gather(weights[0], "segment", axis=0, tiled=False)

    cols = lax.dynamic_index_in_dim(tile_cols, core, 0, keepdims=False)
    count = lax.dynamic_index_in_dim(tile_count, core, 0, keepdims=False)
    relative = (cols - (node - 1) * per_group) % (per_group * groups)
    places = jnp.where(relative < per_group, relative + per_group, jnp.where(relative < 2 * per_group, relative - per_group, relative))
    places = jnp.where(jnp.arange(slots, dtype=jnp.int32)[None, :] < count[:, None], places, 12)

    initial = lax.dynamic_index_in_dim(features, core, 0, keepdims=False)
    held = lax.dynamic_index_in_dim(tiles, core, 0, keepdims=False).reshape(-1, BLOCK, BLOCK)
    to_own, to_before, to_after = dense_adjacency(places, held)

    hidden = initial
    kept = [initial, initial]
    low = seg - core
    for step in range(layers):
        beta = math.log(0.5 / (step + 1) + 1.0)
        before = lax.ppermute(hidden, "node", up)
        after = lax.ppermute(hidden, "node", down)
        part = own_part(to_own, hidden)
        hidden = layer(beta, to_before, to_after, part, before, after, initial, all_weights[step])
        kept[step % 2] = jnp.where(low == step - step % 2, hidden, kept[step % 2])

    mine = jnp.where(core == 0, kept[0], kept[1])
    give = jnp.where(core == 0, kept[1], kept[0])
    other = lax.ppermute(give, "segment", swap)
    first = jnp.where(core == 0, mine, other)
    second = jnp.where(core == 0, other, mine)
    return jnp.stack([first, second])[None]


def solution(mesh):
    in_specs = (
        P(None, "node", None),
        P(None, "node", None, None, None),
        P(None, "node", None),
        P(None, "node"),
        P("segment", None, None),
    )
    out_specs = P("segment", None, "node", None)
    return jax.shard_map(
        on_device, mesh=mesh, in_specs=in_specs, out_specs=out_specs, check_vma=False
    )
```

```python
import math

import jax
import jax.numpy as jnp
from jax import lax
from jax.experimental import pallas as pl
from jax.experimental.pallas import tpu as pltpu
from jax.sharding import PartitionSpec as P

BLOCK = 128
HALF = 256
VMEM = pl.BlockSpec(memory_space=pltpu.VMEM)
SMEM = pl.BlockSpec(memory_space=pltpu.SMEM)


def dense_kernel(places_ref, tiles_ref, own_ref, before_ref, after_ref, total_ref):
    total_ref[...] = jnp.zeros_like(total_ref)
    blocks, slots = places_ref.shape
    for b in range(blocks):
        rows = pl.ds(b * BLOCK, BLOCK)

        @pl.loop(0, slots)
        def _(k):
            place = places_ref[b, k]
            chunk = place // 2
            tile = tiles_ref[b * slots + k].astype(jnp.float32)

            @pl.when((place < 12) & (place % 2 == 0))
            def _():
                total_ref[chunk, rows, 0:BLOCK] += tile

            @pl.when((place < 12) & (place % 2 == 1))
            def _():
                total_ref[chunk, rows, BLOCK:HALF] += tile

    own_ref[...] = total_ref[0:2].astype(jnp.bfloat16)
    before_ref[...] = total_ref[2:4].astype(jnp.bfloat16)
    after_ref[...] = total_ref[4:6].astype(jnp.bfloat16)


def dense_adjacency(places, tiles):
    rows = places.shape[0] * BLOCK
    part = jax.ShapeDtypeStruct((2, rows, HALF), jnp.bfloat16)
    return pl.pallas_call(
        dense_kernel,
        out_shape=(part, part, part),
        in_specs=[SMEM, VMEM],
        out_specs=(VMEM, VMEM, VMEM),
        scratch_shapes=[pltpu.VMEM((6, rows, HALF), jnp.float32)],
        compiler_params=pltpu.CompilerParams(vmem_limit_bytes=16 << 20),
    )(places, tiles)


def product(dense_ref, rows_ref, rows=slice(None)):
    first = jnp.dot(dense_ref[0, rows, :], rows_ref[0:HALF, :], preferred_element_type=jnp.float32)
    second = jnp.dot(dense_ref[1, rows, :], rows_ref[HALF:, :], preferred_element_type=jnp.float32)
    return first + second


def own_kernel(dense_ref, own_ref, part_ref):
    @pl.loop(0, 4)
    def _(r):
        rows = pl.ds(pl.multiple_of(r * BLOCK, BLOCK), BLOCK)
        part_ref[rows, :] = product(dense_ref, own_ref, rows)


def own_part(dense, own):
    return pl.pallas_call(
        own_kernel,
        out_shape=jax.ShapeDtypeStruct(own.shape, jnp.float32),
        in_specs=[VMEM, VMEM],
        out_specs=VMEM,
        compiler_params=pltpu.CompilerParams(vmem_limit_bytes=12 << 20),
        cost_estimate=pl.CostEstimate(flops=2 * 512 * 512 * 256, bytes_accessed=1 << 20, transcendentals=0),
    )(dense, own)


def layer_kernel(beta, to_before_ref, to_after_ref, part_ref, before_ref, after_ref, initial_ref, weight_ref, out_ref):
    aggregate = part_ref[...] + product(to_before_ref, before_ref)
    aggregate = aggregate + product(to_after_ref, after_ref)
    support = (0.9 * aggregate + 0.1 * initial_ref[...].astype(jnp.float32)).astype(jnp.bfloat16)
    branch = jnp.dot(support, weight_ref[...], preferred_element_type=jnp.float32)
    combined = (1.0 - beta) * support.astype(jnp.float32) + beta * branch
    out_ref[...] = jnp.maximum(combined, 0.0).astype(jnp.bfloat16)


def layer(beta, to_before, to_after, part, before, after, initial, weight):
    return pl.pallas_call(
        lambda *refs: layer_kernel(beta, *refs),
        out_shape=jax.ShapeDtypeStruct(initial.shape, jnp.bfloat16),
        in_specs=[VMEM] * 7,
        out_specs=VMEM,
        compiler_params=pltpu.CompilerParams(vmem_limit_bytes=12 << 20),
        cost_estimate=pl.CostEstimate(flops=2 * 512 * 1280 * 256, bytes_accessed=2 << 20, transcendentals=0),
    )(to_before, to_after, part, before, after, initial, weight)


RING = ((0, 0), (0, 1), (1, 1), (2, 1), (3, 1), (3, 0), (2, 0), (1, 0))


def ring_node(span, pair):
    y, x = RING[pair % len(RING)]
    return y * 4 + x + 2 * span


def on_device(features, tiles, tile_cols, tile_count, weights):
    groups = lax.axis_size("node")
    layers = lax.axis_size("segment")
    seg = lax.axis_index("segment")
    node = lax.axis_index("node")
    per_group, slots = tile_cols.shape[1:]
    core = seg % 2
    both = ("segment", "node")
    swap = [(s, s ^ 1) for s in range(layers)]
    gather, across_pairs = [], []
    for plane in range(0, layers, 2):
        for span in range(2):
            for g in range(groups):
                held_at = (plane + g % 2) * groups + ring_node(span, g // 2)
                gather.append(((plane + span) * groups + g, held_at))
                beyond = g + 1 if g % 2 else g + groups - 1
                beyond_at = (plane + beyond % 2) * groups + ring_node(span, beyond % groups // 2)
                across_pairs.append((held_at, beyond_at))
    scatter = [(b, a) for a, b in gather]

    all_weights = lax.all_gather(weights[0], "segment", axis=0, tiled=False)

    cols = lax.dynamic_index_in_dim(tile_cols, core, 0, keepdims=False)
    count = lax.dynamic_index_in_dim(tile_count, core, 0, keepdims=False)
    relative = (cols - (node - 1) * per_group) % (per_group * groups)
    side = relative // per_group
    part_of = jnp.where(side == 1, 0, jnp.where((side == 2) == (node % 2 == 0), 1, 2))
    places = part_of * per_group + relative % per_group
    places = jnp.where(jnp.arange(slots, dtype=jnp.int32)[None, :] < count[:, None], places, 12)
    note = jnp.zeros((16, BLOCK), jnp.bfloat16).at[0:per_group, 0:slots].set(places.astype(jnp.bfloat16))

    mine = lax.dynamic_index_in_dim(features, core, 0, keepdims=False)
    mine_tiles = lax.dynamic_index_in_dim(tiles, core, 0, keepdims=False).reshape(-1, BLOCK)
    bundle = jnp.concatenate([mine_tiles, mine[:, :BLOCK], mine[:, BLOCK:], note], axis=0)
    bundle = lax.ppermute(bundle, both, gather)

    tile_rows = mine_tiles.shape[0]
    rows = mine.shape[0]
    held_tiles = bundle[:tile_rows].reshape(-1, BLOCK, BLOCK)
    initial = jnp.concatenate(
        [bundle[tile_rows : tile_rows + rows], bundle[tile_rows + rows : tile_rows + 2 * rows]], axis=1
    )
    held_places = bundle[tile_rows + 2 * rows :][0:per_group, 0:slots].astype(jnp.int32)
    to_own, to_beside, to_across = dense_adjacency(held_places, held_tiles)

    hidden = initial
    kept = [initial, initial]
    low = seg - core
    for step in range(layers):
        beta = math.log(0.5 / (step + 1) + 1.0)
        across = lax.ppermute(hidden, both, across_pairs)
        beside = lax.ppermute(hidden, "segment", swap)
        part = own_part(to_own, hidden)
        hidden = layer(beta, to_beside, to_across, part, beside, across, initial, all_weights[step])
        kept[step % 2] = jnp.where(low == step - step % 2, hidden, kept[step % 2])

    arrived = [lax.ppermute(value, both, scatter) for value in kept]
    mine_out = jnp.where(core == 0, arrived[0], arrived[1])
    give = jnp.where(core == 0, arrived[1], arrived[0])
    other = lax.ppermute(give, "segment", swap)
    first = jnp.where(core == 0, mine_out, other)
    second = jnp.where(core == 0, other, mine_out)
    return jnp.stack([first, second])[None]


def solution(mesh):
    in_specs = (
        P(None, "node", None),
        P(None, "node", None, None, None),
        P(None, "node", None),
        P(None, "node"),
        P("segment", None, None),
    )
    out_specs = P("segment", None, "node", None)
    return jax.shard_map(
        on_device, mesh=mesh, in_specs=in_specs, out_specs=out_specs, check_vma=False
    )
```

```python
import math

import jax
import jax.numpy as jnp
from jax import lax
from jax.experimental import pallas as pl
from jax.experimental.pallas import tpu as pltpu
from jax.sharding import PartitionSpec as P

BLOCK = 128
HALF = 256
VMEM = pl.BlockSpec(memory_space=pltpu.VMEM)
SMEM = pl.BlockSpec(memory_space=pltpu.SMEM)


def dense_kernel(places_ref, tiles_ref, own_ref, before_ref, after_ref, total_ref):
    total_ref[...] = jnp.zeros_like(total_ref)
    blocks, slots = places_ref.shape
    for b in range(blocks):
        rows = pl.ds(b * BLOCK, BLOCK)

        @pl.loop(0, slots)
        def _(k):
            place = places_ref[b, k]
            chunk = place // 2
            tile = tiles_ref[b * slots + k].astype(jnp.float32)

            @pl.when((place < 12) & (place % 2 == 0))
            def _():
                total_ref[chunk, rows, 0:BLOCK] += tile

            @pl.when((place < 12) & (place % 2 == 1))
            def _():
                total_ref[chunk, rows, BLOCK:HALF] += tile

    own_ref[...] = total_ref[0:2].astype(jnp.bfloat16)
    before_ref[...] = total_ref[2:4].astype(jnp.bfloat16)
    after_ref[...] = total_ref[4:6].astype(jnp.bfloat16)


def dense_adjacency(places, tiles):
    rows = places.shape[0] * BLOCK
    part = jax.ShapeDtypeStruct((2, rows, HALF), jnp.bfloat16)
    return pl.pallas_call(
        dense_kernel,
        out_shape=(part, part, part),
        in_specs=[SMEM, VMEM],
        out_specs=(VMEM, VMEM, VMEM),
        scratch_shapes=[pltpu.VMEM((6, rows, HALF), jnp.float32)],
        compiler_params=pltpu.CompilerParams(vmem_limit_bytes=16 << 20),
    )(places, tiles)


def product(dense_ref, rows_ref, rows=slice(None)):
    first = jnp.dot(dense_ref[0, rows, :], rows_ref[0:HALF, :], preferred_element_type=jnp.float32)
    second = jnp.dot(dense_ref[1, rows, :], rows_ref[HALF:, :], preferred_element_type=jnp.float32)
    return first + second


def own_kernel(dense_ref, own_ref, part_ref):
    @pl.loop(0, 4)
    def _(r):
        rows = pl.ds(pl.multiple_of(r * BLOCK, BLOCK), BLOCK)
        part_ref[rows, :] = product(dense_ref, own_ref, rows)


def own_part(dense, own):
    return pl.pallas_call(
        own_kernel,
        out_shape=jax.ShapeDtypeStruct(own.shape, jnp.float32),
        in_specs=[VMEM, VMEM],
        out_specs=VMEM,
        compiler_params=pltpu.CompilerParams(vmem_limit_bytes=12 << 20),
        cost_estimate=pl.CostEstimate(flops=2 * 512 * 512 * 256, bytes_accessed=1 << 20, transcendentals=0),
    )(dense, own)


def layer_kernel(beta, to_before_ref, to_after_ref, part_ref, before_ref, after_ref, initial_ref, weight_ref, out_ref):
    aggregate = part_ref[...] + product(to_before_ref, before_ref)
    aggregate = aggregate + product(to_after_ref, after_ref)
    support = (0.9 * aggregate + 0.1 * initial_ref[...].astype(jnp.float32)).astype(jnp.bfloat16)
    branch = jnp.dot(support, weight_ref[...], preferred_element_type=jnp.float32)
    combined = (1.0 - beta) * support.astype(jnp.float32) + beta * branch
    out_ref[...] = jnp.maximum(combined, 0.0).astype(jnp.bfloat16)


def layer(beta, to_before, to_after, part, before, after, initial, weight):
    return pl.pallas_call(
        lambda *refs: layer_kernel(beta, *refs),
        out_shape=jax.ShapeDtypeStruct(initial.shape, jnp.bfloat16),
        in_specs=[VMEM] * 7,
        out_specs=VMEM,
        compiler_params=pltpu.CompilerParams(vmem_limit_bytes=12 << 20),
        cost_estimate=pl.CostEstimate(flops=2 * 512 * 1280 * 256, bytes_accessed=2 << 20, transcendentals=0),
    )(to_before, to_after, part, before, after, initial, weight)


RINGS = (
    ((1, 0), (0, 0), (0, 1), (1, 1), (2, 1), (3, 1), (3, 0), (2, 0)),
    ((1, 2), (0, 2), (0, 3), (1, 3), (2, 3), (3, 3), (3, 2), (2, 2)),
)


def ring_node(span, pair):
    y, x = RINGS[span][pair % 8]
    return y * 4 + x


def on_device(features, tiles, tile_cols, tile_count, weights):
    groups = lax.axis_size("node")
    layers = lax.axis_size("segment")
    seg = lax.axis_index("segment")
    node = lax.axis_index("node")
    per_group, slots = tile_cols.shape[1:]
    core = seg % 2
    both = ("segment", "node")
    swap = [(s, s ^ 1) for s in range(layers)]
    gather, across_pairs = [], []
    for plane in range(0, layers, 2):
        for span in range(2):
            for g in range(groups):
                held_at = (plane + g % 2) * groups + ring_node(span, g // 2)
                gather.append(((plane + span) * groups + g, held_at))
                beyond = g + 1 if g % 2 else g + groups - 1
                beyond_at = (plane + beyond % 2) * groups + ring_node(span, beyond % groups // 2)
                across_pairs.append((held_at, beyond_at))
    scatter = [(b, a) for a, b in gather]

    all_weights = lax.all_gather(weights[0], "segment", axis=0, tiled=False)

    cols = lax.dynamic_index_in_dim(tile_cols, core, 0, keepdims=False)
    count = lax.dynamic_index_in_dim(tile_count, core, 0, keepdims=False)
    relative = (cols - (node - 1) * per_group) % (per_group * groups)
    side = relative // per_group
    part_of = jnp.where(side == 1, 0, jnp.where((side == 2) == (node % 2 == 0), 1, 2))
    places = part_of * per_group + relative % per_group
    places = jnp.where(jnp.arange(slots, dtype=jnp.int32)[None, :] < count[:, None], places, 12)
    note = jnp.zeros((16, BLOCK), jnp.bfloat16).at[0:per_group, 0:slots].set(places.astype(jnp.bfloat16))

    mine = lax.dynamic_index_in_dim(features, core, 0, keepdims=False)
    mine_tiles = lax.dynamic_index_in_dim(tiles, core, 0, keepdims=False).reshape(-1, BLOCK)
    bundle = jnp.concatenate([mine_tiles, mine[:, :BLOCK], mine[:, BLOCK:], note], axis=0)
    bundle = lax.ppermute(bundle, both, gather)

    tile_rows = mine_tiles.shape[0]
    rows = mine.shape[0]
    held_tiles = bundle[:tile_rows].reshape(-1, BLOCK, BLOCK)
    initial = jnp.concatenate(
        [bundle[tile_rows : tile_rows + rows], bundle[tile_rows + rows : tile_rows + 2 * rows]], axis=1
    )
    held_places = bundle[tile_rows + 2 * rows :][0:per_group, 0:slots].astype(jnp.int32)
    to_own, to_beside, to_across = dense_adjacency(held_places, held_tiles)

    hidden = initial
    kept = [initial, initial]
    low = seg - core
    for step in range(layers):
        beta = math.log(0.5 / (step + 1) + 1.0)
        across = lax.ppermute(hidden, both, across_pairs)
        beside = lax.ppermute(hidden, "segment", swap)
        part = own_part(to_own, hidden)
        hidden = layer(beta, to_beside, to_across, part, beside, across, initial, all_weights[step])
        kept[step % 2] = jnp.where(low == step - step % 2, hidden, kept[step % 2])

    arrived = [lax.ppermute(value, both, scatter) for value in kept]
    mine_out = jnp.where(core == 0, arrived[0], arrived[1])
    give = jnp.where(core == 0, arrived[1], arrived[0])
    other = lax.ppermute(give, "segment", swap)
    first = jnp.where(core == 0, mine_out, other)
    second = jnp.where(core == 0, other, mine_out)
    return jnp.stack([first, second])[None]


def solution(mesh):
    in_specs = (
        P(None, "node", None),
        P(None, "node", None, None, None),
        P(None, "node", None),
        P(None, "node"),
        P("segment", None, None),
    )
    out_specs = P("segment", None, "node", None)
    return jax.shard_map(
        on_device, mesh=mesh, in_specs=in_specs, out_specs=out_specs, check_vma=False
    )
```

```python
import math

import jax
import jax.numpy as jnp
from jax import lax
from jax.experimental import pallas as pl
from jax.experimental.pallas import tpu as pltpu
from jax.sharding import PartitionSpec as P

BLOCK = 128
HALF = 256
VMEM = pl.BlockSpec(memory_space=pltpu.VMEM)
SMEM = pl.BlockSpec(memory_space=pltpu.SMEM)


def dense_kernel(places_ref, tiles_ref, own_ref, before_ref, after_ref, total_ref):
    total_ref[...] = jnp.zeros_like(total_ref)
    blocks, slots = places_ref.shape
    for b in range(blocks):
        rows = pl.ds(b * BLOCK, BLOCK)

        @pl.loop(0, slots)
        def _(k):
            place = places_ref[b, k]
            chunk = place // 2
            tile = tiles_ref[b * slots + k].astype(jnp.float32)

            @pl.when((place < 12) & (place % 2 == 0))
            def _():
                total_ref[chunk, rows, 0:BLOCK] += tile

            @pl.when((place < 12) & (place % 2 == 1))
            def _():
                total_ref[chunk, rows, BLOCK:HALF] += tile

    own_ref[...] = total_ref[0:2].astype(jnp.bfloat16)
    before_ref[...] = total_ref[2:4].astype(jnp.bfloat16)
    after_ref[...] = total_ref[4:6].astype(jnp.bfloat16)


def dense_adjacency(places, tiles):
    rows = places.shape[0] * BLOCK
    part = jax.ShapeDtypeStruct((2, rows, HALF), jnp.bfloat16)
    return pl.pallas_call(
        dense_kernel,
        out_shape=(part, part, part),
        in_specs=[SMEM, VMEM],
        out_specs=(VMEM, VMEM, VMEM),
        scratch_shapes=[pltpu.VMEM((6, rows, HALF), jnp.float32)],
        compiler_params=pltpu.CompilerParams(vmem_limit_bytes=16 << 20),
    )(places, tiles)


def product(dense_ref, rows_ref, rows=slice(None)):
    first = jnp.dot(dense_ref[0, rows, :], rows_ref[0:HALF, :], preferred_element_type=jnp.float32)
    second = jnp.dot(dense_ref[1, rows, :], rows_ref[HALF:, :], preferred_element_type=jnp.float32)
    return first + second


def near_kernel(to_own_ref, to_beside_ref, own_ref, beside_ref, part_ref):
    @pl.loop(0, 4)
    def _(r):
        rows = pl.ds(pl.multiple_of(r * BLOCK, BLOCK), BLOCK)
        part_ref[rows, :] = product(to_own_ref, own_ref, rows) + product(to_beside_ref, beside_ref, rows)


def near_part(to_own, to_beside, own, beside):
    return pl.pallas_call(
        near_kernel,
        out_shape=jax.ShapeDtypeStruct(own.shape, jnp.float32),
        in_specs=[VMEM] * 4,
        out_specs=VMEM,
        compiler_params=pltpu.CompilerParams(vmem_limit_bytes=8 << 20),
        cost_estimate=pl.CostEstimate(flops=2 * 512 * 1024 * 256, bytes_accessed=2 << 20, transcendentals=0),
    )(to_own, to_beside, own, beside)


def layer_kernel(beta, to_across_ref, part_ref, across_ref, initial_ref, weight_ref, out_ref):
    aggregate = part_ref[...] + product(to_across_ref, across_ref)
    support = (0.9 * aggregate + 0.1 * initial_ref[...].astype(jnp.float32)).astype(jnp.bfloat16)
    branch = jnp.dot(support, weight_ref[...], preferred_element_type=jnp.float32)
    combined = (1.0 - beta) * support.astype(jnp.float32) + beta * branch
    out_ref[...] = jnp.maximum(combined, 0.0).astype(jnp.bfloat16)


def layer(beta, to_across, part, across, initial, weight):
    return pl.pallas_call(
        lambda *refs: layer_kernel(beta, *refs),
        out_shape=jax.ShapeDtypeStruct(initial.shape, jnp.bfloat16),
        in_specs=[VMEM] * 5,
        out_specs=VMEM,
        compiler_params=pltpu.CompilerParams(vmem_limit_bytes=8 << 20),
        cost_estimate=pl.CostEstimate(flops=2 * 512 * 768 * 256, bytes_accessed=2 << 20, transcendentals=0),
    )(to_across, part, across, initial, weight)


RINGS = (
    ((1, 0), (0, 0), (0, 1), (1, 1), (2, 1), (3, 1), (3, 0), (2, 0)),
    ((1, 2), (0, 2), (0, 3), (1, 3), (2, 3), (3, 3), (3, 2), (2, 2)),
)


def ring_node(span, pair):
    y, x = RINGS[span][pair % 8]
    return y * 4 + x


def on_device(features, tiles, tile_cols, tile_count, weights):
    groups = lax.axis_size("node")
    layers = lax.axis_size("segment")
    seg = lax.axis_index("segment")
    node = lax.axis_index("node")
    per_group, slots = tile_cols.shape[1:]
    core = seg % 2
    both = ("segment", "node")
    swap = [(s, s ^ 1) for s in range(layers)]
    gather, across_pairs = [], []
    for plane in range(0, layers, 2):
        for span in range(2):
            for g in range(groups):
                held_at = (plane + g % 2) * groups + ring_node(span, g // 2)
                gather.append(((plane + span) * groups + g, held_at))
                beyond = g + 1 if g % 2 else g + groups - 1
                beyond_at = (plane + beyond % 2) * groups + ring_node(span, beyond % groups // 2)
                across_pairs.append((held_at, beyond_at))
    scatter = [(b, a) for a, b in gather]

    all_weights = lax.all_gather(weights[0], "segment", axis=0, tiled=False)

    cols = lax.dynamic_index_in_dim(tile_cols, core, 0, keepdims=False)
    count = lax.dynamic_index_in_dim(tile_count, core, 0, keepdims=False)
    relative = (cols - (node - 1) * per_group) % (per_group * groups)
    side = relative // per_group
    part_of = jnp.where(side == 1, 0, jnp.where((side == 2) == (node % 2 == 0), 1, 2))
    places = part_of * per_group + relative % per_group
    places = jnp.where(jnp.arange(slots, dtype=jnp.int32)[None, :] < count[:, None], places, 12)
    note = jnp.zeros((16, BLOCK), jnp.bfloat16).at[0:per_group, 0:slots].set(places.astype(jnp.bfloat16))

    initial = lax.ppermute(lax.dynamic_index_in_dim(features, core, 0, keepdims=False), both, gather)
    mine_tiles = lax.dynamic_index_in_dim(tiles, core, 0, keepdims=False).reshape(-1, BLOCK)
    bundle = lax.ppermute(jnp.concatenate([mine_tiles, note], axis=0), both, gather)

    tile_rows = mine_tiles.shape[0]
    held_tiles = bundle[:tile_rows].reshape(-1, BLOCK, BLOCK)
    held_places = bundle[tile_rows:][0:per_group, 0:slots].astype(jnp.int32)
    to_own, to_beside, to_across = dense_adjacency(held_places, held_tiles)

    hidden = initial
    kept = [initial, initial]
    low = seg - core
    for step in range(layers):
        beta = math.log(0.5 / (step + 1) + 1.0)
        all_weights, hidden = lax.optimization_barrier((all_weights, hidden)) if step else (all_weights, hidden)
        across = lax.ppermute(hidden, both, across_pairs)
        beside = lax.ppermute(hidden, "segment", swap)
        part = near_part(to_own, to_beside, hidden, beside)
        hidden = layer(beta, to_across, part, across, initial, all_weights[step])
        kept[step % 2] = jnp.where(low == step - step % 2, hidden, kept[step % 2])

    arrived = [lax.ppermute(value, both, scatter) for value in kept]
    mine_out = jnp.where(core == 0, arrived[0], arrived[1])
    give = jnp.where(core == 0, arrived[1], arrived[0])
    other = lax.ppermute(give, "segment", swap)
    result = jnp.zeros((1,) + features.shape, jnp.bfloat16)
    result = lax.dynamic_update_slice(result, mine_out[None, None], (0, core, 0, 0))
    return lax.dynamic_update_slice(result, other[None, None], (0, 1 - core, 0, 0))


def solution(mesh):
    in_specs = (
        P(None, "node", None),
        P(None, "node", None, None, None),
        P(None, "node", None),
        P(None, "node"),
        P("segment", None, None),
    )
    out_specs = P("segment", None, "node", None)
    return jax.shard_map(
        on_device, mesh=mesh, in_specs=in_specs, out_specs=out_specs, check_vma=False
    )
```

```python
import math

import jax
import jax.numpy as jnp
from jax import lax
from jax.experimental import pallas as pl
from jax.experimental.pallas import tpu as pltpu
from jax.sharding import PartitionSpec as P

BLOCK = 128
HALF = 256
VMEM = pl.BlockSpec(memory_space=pltpu.VMEM)
SMEM = pl.BlockSpec(memory_space=pltpu.SMEM)


def dense_kernel(places_ref, tiles_ref, own_ref, before_ref, after_ref, total_ref):
    total_ref[...] = jnp.zeros_like(total_ref)
    blocks, slots = places_ref.shape
    for b in range(blocks):
        rows = pl.ds(b * BLOCK, BLOCK)

        @pl.loop(0, slots)
        def _(k):
            place = places_ref[b, k]
            chunk = place // 2
            tile = tiles_ref[b * slots + k].astype(jnp.float32)

            @pl.when((place < 12) & (place % 2 == 0))
            def _():
                total_ref[chunk, rows, 0:BLOCK] += tile

            @pl.when((place < 12) & (place % 2 == 1))
            def _():
                total_ref[chunk, rows, BLOCK:HALF] += tile

    own_ref[...] = total_ref[0:2].astype(jnp.bfloat16)
    before_ref[...] = total_ref[2:4].astype(jnp.bfloat16)
    after_ref[...] = total_ref[4:6].astype(jnp.bfloat16)


def dense_adjacency(places, tiles):
    rows = places.shape[0] * BLOCK
    part = jax.ShapeDtypeStruct((2, rows, HALF), jnp.bfloat16)
    return pl.pallas_call(
        dense_kernel,
        out_shape=(part, part, part),
        in_specs=[SMEM, VMEM],
        out_specs=(VMEM, VMEM, VMEM),
        scratch_shapes=[pltpu.VMEM((6, rows, HALF), jnp.float32)],
        compiler_params=pltpu.CompilerParams(vmem_limit_bytes=16 << 20),
    )(places, tiles)


def product(dense_ref, rows_ref, rows=slice(None)):
    first = jnp.dot(dense_ref[0, rows, :], rows_ref[0:HALF, :], preferred_element_type=jnp.float32)
    second = jnp.dot(dense_ref[1, rows, :], rows_ref[HALF:, :], preferred_element_type=jnp.float32)
    return first + second


def near_kernel(to_own_ref, to_beside_ref, own_ref, beside_ref, part_ref):
    @pl.loop(0, 4)
    def _(r):
        rows = pl.ds(pl.multiple_of(r * BLOCK, BLOCK), BLOCK)
        part_ref[rows, :] = product(to_own_ref, own_ref, rows) + product(to_beside_ref, beside_ref, rows)


def near_part(to_own, to_beside, own, beside):
    return pl.pallas_call(
        near_kernel,
        out_shape=jax.ShapeDtypeStruct(own.shape, jnp.float32),
        in_specs=[VMEM] * 4,
        out_specs=VMEM,
        compiler_params=pltpu.CompilerParams(vmem_limit_bytes=8 << 20),
        cost_estimate=pl.CostEstimate(flops=2 * 512 * 1024 * 256, bytes_accessed=2 << 20, transcendentals=0),
    )(to_own, to_beside, own, beside)


def layer_kernel(beta, to_across_ref, part_ref, across_ref, initial_ref, weight_ref, out_ref):
    aggregate = part_ref[...] + product(to_across_ref, across_ref)
    support = (0.9 * aggregate + 0.1 * initial_ref[...].astype(jnp.float32)).astype(jnp.bfloat16)
    branch = jnp.dot(support, weight_ref[...], preferred_element_type=jnp.float32)
    combined = (1.0 - beta) * support.astype(jnp.float32) + beta * branch
    out_ref[...] = jnp.maximum(combined, 0.0).astype(jnp.bfloat16)


def layer(beta, to_across, part, across, initial, weight):
    return pl.pallas_call(
        lambda *refs: layer_kernel(beta, *refs),
        out_shape=jax.ShapeDtypeStruct(initial.shape, jnp.bfloat16),
        in_specs=[VMEM] * 5,
        out_specs=VMEM,
        compiler_params=pltpu.CompilerParams(vmem_limit_bytes=8 << 20),
        cost_estimate=pl.CostEstimate(flops=2 * 512 * 768 * 256, bytes_accessed=2 << 20, transcendentals=0),
    )(to_across, part, across, initial, weight)


RINGS = (
    ((1, 0), (0, 0), (0, 1), (1, 1), (2, 1), (3, 1), (3, 0), (2, 0)),
    ((1, 2), (0, 2), (0, 3), (1, 3), (2, 3), (3, 3), (3, 2), (2, 2)),
)


def ring_node(span, pair):
    y, x = RINGS[span][pair % 8]
    return y * 4 + x


def on_device(features, tiles, tile_cols, tile_count, weights):
    groups = lax.axis_size("node")
    layers = lax.axis_size("segment")
    seg = lax.axis_index("segment")
    node = lax.axis_index("node")
    per_group, slots = tile_cols.shape[1:]
    core = seg % 2
    both = ("segment", "node")
    swap = [(s, s ^ 1) for s in range(layers)]
    gather, across_pairs = [], []
    for plane in range(0, layers, 2):
        for span in range(2):
            for g in range(groups):
                held_at = (plane + g % 2) * groups + ring_node(span, g // 2)
                gather.append(((plane + span) * groups + g, held_at))
                beyond = g + 1 if g % 2 else g + groups - 1
                beyond_at = (plane + beyond % 2) * groups + ring_node(span, beyond % groups // 2)
                across_pairs.append((held_at, beyond_at))
    scatter = [(b, a) for a, b in gather]

    cols = lax.dynamic_index_in_dim(tile_cols, core, 0, keepdims=False)
    count = lax.dynamic_index_in_dim(tile_count, core, 0, keepdims=False)
    relative = (cols - (node - 1) * per_group) % (per_group * groups)
    side = relative // per_group
    part_of = jnp.where(side == 1, 0, jnp.where((side == 2) == (node % 2 == 0), 1, 2))
    places = part_of * per_group + relative % per_group
    places = jnp.where(jnp.arange(slots, dtype=jnp.int32)[None, :] < count[:, None], places, 12)
    note = jnp.zeros((16, features.shape[-1]), jnp.bfloat16).at[0:per_group, 0:slots].set(places.astype(jnp.bfloat16))

    mine_tiles = lax.dynamic_index_in_dim(tiles, core, 0, keepdims=False)
    held_tiles = lax.ppermute(mine_tiles.reshape(-1, BLOCK, BLOCK), both, gather)
    rows = features.shape[1]
    bundle = jnp.concatenate([lax.dynamic_index_in_dim(features, core, 0, keepdims=False), note], axis=0)
    bundle = lax.ppermute(bundle, both, gather)
    initial = bundle[:rows]
    held_places = bundle[rows:][0:per_group, 0:slots].astype(jnp.int32)

    planes = layers // 2
    forward = [(s, (s + 2) % layers) for s in range(layers)]
    backward = [(b, a) for a, b in forward]
    from_below = from_above = weights[0]
    below, above = [], []
    for turn in range(planes // 2):
        if turn == 1:
            from_below, from_above, initial = lax.optimization_barrier((from_below, from_above, initial))
        from_below = lax.ppermute(from_below, "segment", forward)
        below.append(from_below)
        if turn < planes // 2 - 1:
            from_above = lax.ppermute(from_above, "segment", backward)
            above.append(from_above)
    of_mine = [weights[0]] + above + below[::-1]
    of_other = [lax.ppermute(value, "segment", swap) for value in of_mine]

    def weight_of(step, of_mine, of_other):
        place = (step // 2 - seg // 2) % planes
        chosen = jnp.where(core == step % 2, of_mine[0], of_other[0])
        for d in range(1, planes):
            chosen = jnp.where(place == d, jnp.where(core == step % 2, of_mine[d], of_other[d]), chosen)
        return chosen

    to_own, to_beside, to_across = dense_adjacency(held_places, held_tiles)

    hidden = initial
    kept = [initial, initial]
    low = seg - core
    for step in range(layers):
        beta = math.log(0.5 / (step + 1) + 1.0)
        if step:
            of_mine, of_other, hidden = lax.optimization_barrier((of_mine, of_other, hidden))
        across = lax.ppermute(hidden, both, across_pairs)
        beside = lax.ppermute(hidden, "segment", swap)
        part = near_part(to_own, to_beside, hidden, beside)
        hidden = layer(beta, to_across, part, across, initial, weight_of(step, of_mine, of_other))
        kept[step % 2] = jnp.where(low == step - step % 2, hidden, kept[step % 2])

    arrived = [lax.ppermute(value, both, scatter) for value in kept]
    mine_out = jnp.where(core == 0, arrived[0], arrived[1])
    give = jnp.where(core == 0, arrived[1], arrived[0])
    other = lax.ppermute(give, "segment", swap)
    result = jnp.zeros((1,) + features.shape, jnp.bfloat16)
    result = lax.dynamic_update_slice(result, mine_out[None, None], (0, core, 0, 0))
    return lax.dynamic_update_slice(result, other[None, None], (0, 1 - core, 0, 0))


def solution(mesh):
    in_specs = (
        P(None, "node", None),
        P(None, "node", None, None, None),
        P(None, "node", None),
        P(None, "node"),
        P("segment", None, None),
    )
    out_specs = P("segment", None, "node", None)
    return jax.shard_map(
        on_device, mesh=mesh, in_specs=in_specs, out_specs=out_specs, check_vma=False
    )
```

```python
import math

import jax
import jax.numpy as jnp
from jax import lax
from jax.experimental import pallas as pl
from jax.experimental.pallas import tpu as pltpu
from jax.sharding import PartitionSpec as P

BLOCK = 128
HALF = 256
VMEM = pl.BlockSpec(memory_space=pltpu.VMEM)
SMEM = pl.BlockSpec(memory_space=pltpu.SMEM)


def dense_kernel(places_ref, tiles_ref, own_ref, before_ref, after_ref, total_ref):
    @pl.loop(0, 6)
    def _(i):
        total_ref[i] = jnp.zeros(total_ref.shape[1:], jnp.float32)

    blocks, slots = places_ref.shape
    @pl.loop(0, blocks * slots)
    def _(t):
        place = places_ref[t // slots, t % slots]
        chunk = place // 2
        rows = pl.ds(pl.multiple_of(t // slots * BLOCK, BLOCK), BLOCK)
        tile = tiles_ref[t].astype(jnp.float32)

        @pl.when((place < 12) & (place % 2 == 0))
        def _():
            total_ref[chunk, rows, 0:BLOCK] += tile

        @pl.when((place < 12) & (place % 2 == 1))
        def _():
            total_ref[chunk, rows, BLOCK:HALF] += tile

    @pl.loop(0, 2)
    def _(i):
        own_ref[i] = total_ref[i].astype(jnp.bfloat16)
        before_ref[i] = total_ref[2 + i].astype(jnp.bfloat16)
        after_ref[i] = total_ref[4 + i].astype(jnp.bfloat16)


def dense_adjacency(places, tiles):
    rows = places.shape[0] * BLOCK
    part = jax.ShapeDtypeStruct((2, rows, HALF), jnp.bfloat16)
    return pl.pallas_call(
        dense_kernel,
        out_shape=(part, part, part),
        in_specs=[SMEM, VMEM],
        out_specs=(VMEM, VMEM, VMEM),
        scratch_shapes=[pltpu.VMEM((6, rows, HALF), jnp.float32)],
        compiler_params=pltpu.CompilerParams(vmem_limit_bytes=16 << 20),
    )(places, tiles)


def product(dense_ref, rows_ref, rows=slice(None)):
    first = jnp.dot(dense_ref[0, rows, :], rows_ref[0:HALF, :], preferred_element_type=jnp.float32)
    second = jnp.dot(dense_ref[1, rows, :], rows_ref[HALF:, :], preferred_element_type=jnp.float32)
    return first + second


def near_kernel(to_own_ref, to_beside_ref, own_ref, beside_ref, part_ref):
    @pl.loop(0, 8)
    def _(r):
        rows = pl.ds(pl.multiple_of(r * 64, 64), 64)
        part_ref[rows, :] = product(to_own_ref, own_ref, rows) + product(to_beside_ref, beside_ref, rows)


def near_part(to_own, to_beside, own, beside):
    return pl.pallas_call(
        near_kernel,
        out_shape=jax.ShapeDtypeStruct(own.shape, jnp.float32),
        in_specs=[VMEM] * 4,
        out_specs=VMEM,
        compiler_params=pltpu.CompilerParams(vmem_limit_bytes=8 << 20),
        cost_estimate=pl.CostEstimate(flops=2 * 512 * 1024 * 256, bytes_accessed=2 << 20, transcendentals=0),
    )(to_own, to_beside, own, beside)


def layer_kernel(beta, to_across_ref, part_ref, across_ref, initial_ref, weight_ref, out_ref):
    aggregate = part_ref[...] + product(to_across_ref, across_ref)
    support = (0.9 * aggregate + 0.1 * initial_ref[...].astype(jnp.float32)).astype(jnp.bfloat16)
    branch = jnp.dot(support, weight_ref[...], preferred_element_type=jnp.float32)
    combined = (1.0 - beta) * support.astype(jnp.float32) + beta * branch
    out_ref[...] = jnp.maximum(combined, 0.0).astype(jnp.bfloat16)


def layer(beta, to_across, part, across, initial, weight):
    return pl.pallas_call(
        lambda *refs: layer_kernel(beta, *refs),
        out_shape=jax.ShapeDtypeStruct(initial.shape, jnp.bfloat16),
        in_specs=[VMEM] * 5,
        out_specs=VMEM,
        compiler_params=pltpu.CompilerParams(vmem_limit_bytes=8 << 20),
        cost_estimate=pl.CostEstimate(flops=2 * 512 * 768 * 256, bytes_accessed=2 << 20, transcendentals=0),
    )(to_across, part, across, initial, weight)


RINGS = (
    ((1, 0), (0, 0), (0, 1), (1, 1), (2, 1), (3, 1), (3, 0), (2, 0)),
    ((1, 2), (0, 2), (0, 3), (1, 3), (2, 3), (3, 3), (3, 2), (2, 2)),
)


def ring_node(span, pair):
    y, x = RINGS[span][pair % 8]
    return y * 4 + x


def on_device(features, tiles, tile_cols, tile_count, weights):
    groups = lax.axis_size("node")
    layers = lax.axis_size("segment")
    seg = lax.axis_index("segment")
    node = lax.axis_index("node")
    per_group, slots = tile_cols.shape[1:]
    core = seg % 2
    both = ("segment", "node")
    swap = [(s, s ^ 1) for s in range(layers)]
    gather, across_pairs = [], []
    for plane in range(0, layers, 2):
        for span in range(2):
            for g in range(groups):
                held_at = (plane + g % 2) * groups + ring_node(span, g // 2)
                gather.append(((plane + span) * groups + g, held_at))
                beyond = g + 1 if g % 2 else g + groups - 1
                beyond_at = (plane + beyond % 2) * groups + ring_node(span, beyond % groups // 2)
                across_pairs.append((held_at, beyond_at))
    scatter = [(b, a) for a, b in gather]

    cols = lax.dynamic_index_in_dim(tile_cols, core, 0, keepdims=False)
    count = lax.dynamic_index_in_dim(tile_count, core, 0, keepdims=False)
    relative = (cols - (node - 1) * per_group) % (per_group * groups)
    side = relative // per_group
    part_of = jnp.where(side == 1, 0, jnp.where((side == 2) == (node % 2 == 0), 1, 2))
    places = part_of * per_group + relative % per_group
    places = jnp.where(jnp.arange(slots, dtype=jnp.int32)[None, :] < count[:, None], places, 12)
    note = jnp.zeros((16, features.shape[-1]), jnp.bfloat16).at[0:per_group, 0:slots].set(places.astype(jnp.bfloat16))

    mine_tiles = lax.dynamic_index_in_dim(tiles, core, 0, keepdims=False)
    held_tiles = lax.ppermute(mine_tiles.reshape(-1, BLOCK, BLOCK), both, gather)
    rows = features.shape[1]
    bundle = jnp.concatenate([lax.dynamic_index_in_dim(features, core, 0, keepdims=False), note], axis=0)
    bundle = lax.ppermute(bundle, both, gather)
    initial = bundle[:rows]
    held_places = bundle[rows:][0:per_group, 0:slots].astype(jnp.int32)

    planes = layers // 2
    forward = [(s, (s + 2) % layers) for s in range(layers)]
    backward = [(b, a) for a, b in forward]
    beside_weight = lax.ppermute(weights, "segment", swap)
    from_below = from_above = own_pair = jnp.concatenate([weights, beside_weight], axis=0)
    below, above = [], []
    for turn in range(planes // 2):
        if turn == 1:
            from_below, from_above, initial = lax.optimization_barrier((from_below, from_above, initial))
        from_below = lax.ppermute(from_below, "segment", forward)
        below.append(from_below)
        if turn < planes // 2 - 1:
            from_above = lax.ppermute(from_above, "segment", backward)
            above.append(from_above)
    pairs = [own_pair] + above + below[::-1]

    def weight_of(step, pairs):
        place = (step // 2 - seg // 2) % planes
        chosen = pairs[0]
        for d in range(1, planes):
            chosen = jnp.where(place == d, pairs[d], chosen)
        return jnp.where(core == step % 2, chosen[0], chosen[1])

    to_own, to_beside, to_across = dense_adjacency(held_places, held_tiles)

    hidden = initial
    kept = [initial, initial]
    low = seg - core
    for step in range(layers):
        beta = math.log(0.5 / (step + 1) + 1.0)
        if step:
            pairs, hidden = lax.optimization_barrier((pairs, hidden))
        across = lax.ppermute(hidden, both, across_pairs)
        beside = lax.ppermute(hidden, "segment", swap)
        part = near_part(to_own, to_beside, hidden, beside)
        hidden = layer(beta, to_across, part, across, initial, weight_of(step, pairs))
        kept[step % 2] = jnp.where(low == step - step % 2, hidden, kept[step % 2])

    arrived = [lax.ppermute(value, both, scatter) for value in kept]
    mine_out = jnp.where(core == 0, arrived[0], arrived[1])
    give = jnp.where(core == 0, arrived[1], arrived[0])
    other = lax.ppermute(give, "segment", swap)
    result = jnp.zeros((1,) + features.shape, jnp.bfloat16)
    result = lax.dynamic_update_slice(result, mine_out[None, None], (0, core, 0, 0))
    return lax.dynamic_update_slice(result, other[None, None], (0, 1 - core, 0, 0))


def solution(mesh):
    in_specs = (
        P(None, "node", None),
        P(None, "node", None, None, None),
        P(None, "node", None),
        P(None, "node"),
        P("segment", None, None),
    )
    out_specs = P("segment", None, "node", None)
    return jax.shard_map(
        on_device, mesh=mesh, in_specs=in_specs, out_specs=out_specs, check_vma=False
    )
```
